256 devices in a mesh: group: 4 (over z_hi), dp: 8 (over y, z_lo), mp: 8 (over x, core).
Axes of the slice: x: 4, y: 4, z: 8 (z_hi: 4, z_lo: 2; z = z_hi * 2 + z_lo), core: 2. Of those that a mesh axis runs over, the one named last changes fastest.
Arguments:
- inner_columns: float32 [4, 576, 4032], P('group', None, 'mp'), may hold values from -6 to 6
- inner_rows: float32 [4, 2112, 576], P('group', 'mp'), may hold values from -6 to 6
- inner_norms: float32 [4, 3, 576], P('group'), may hold values from -6 to 6
- inner_embed: float32 [4, 8192, 576], P('group', 'mp'), may hold values from -6 to 6
- basis: float32 [576, 64], replicated, may hold values from -0.25 to 0.25
- outer_layer: float32 [8, 442368], P('mp', ('group', 'dp')), may hold values from -6 to 6
- outer_norms: float32 [1728], P(('group', 'dp')), may hold values from -6 to 6
- outer_embed: float32 [8, 1024, 576], P('mp', ('group', 'dp')), may hold values from -6 to 6
- layer_momentum: float32 [8, 442368], P('mp', ('group', 'dp')), may hold values from -6 to 6
- norm_momentum: float32 [1728], P(('group', 'dp')), may hold values from -6 to 6
- embed_momentum: float32 [8, 1024, 576], P('mp', ('group', 'dp')), may hold values from -6 to 6
Outputs:
- new_columns: float32 [576, 4032], P(None, 'mp')
- new_rows: float32 [2112, 576], P('mp')
- new_norms: float32 [3, 576], replicated
- new_embed: float32 [8192, 576], P('mp')
- new_layer_momentum: float32 [8, 442368], P('mp', ('group', 'dp'))
- new_norm_momentum: float32 [1728], P(('group', 'dp'))
- new_embed_momentum: float32 [8, 1024, 576], P('mp', ('group', 'dp'))
The draws below stay inside these ranges and needn't reach their ends.
All inputs are finite; a program needn't handle non-finite values.
Results may differ from the reference program's by a relative error of at most 0.000076.
Values sent between devices are 32-bit elements; how exact they have to be, the bound alone decides.
No kernel may reach another device: no remote copies, remote signals or barrier semaphores. Data moves between devices by JAX's collectives and lax.ppermute only.
A program may use at most 64 MiB of HBM per device.

```python
import jax
import jax.numpy as jnp
from jax import lax

D = 576
RANK = 64
GROUPS = 4
VOCAB = 8192
IN_COLS = 4032
OUT_ROWS = 2112
LAYER_FLAT = 442368
N_GROUP = 4
N_MP = 8


def block_scale(stream_key, extent, pieces, least, high):
    loudness, own = 1.0, jax.random.fold_in(stream_key, 6)
    for axis_at, shards_of in pieces:
        draws = jnp.exp(jax.random.uniform(jax.random.fold_in(own, axis_at), (shards_of,), jnp.float32, least / len(pieces), high / len(pieces)))
        loudness = loudness * jnp.repeat(draws, extent[axis_at] // shards_of).reshape([-1 if axis == axis_at else 1 for axis in range(len(extent))])
    return loudness


def bell_draw(rng, dims, scale, most, pieces=(), dtype=jnp.bfloat16):
    factor_of = block_scale(rng, dims, pieces, -0.22, 0.18) if pieces else 1.0
    entries = jax.random.normal(rng, dims, jnp.float32) * scale * factor_of
    return jnp.minimum(jnp.maximum(entries, -most), most).astype(dtype)


def setup_inputs(seed: int = 0) -> dict:
    streams_of = jax.random.split(jax.random.key(seed), 12)
    return {
        "inner_columns": bell_draw(streams_of[0], (GROUPS, D, IN_COLS), 1.0, 6.0, ((0, 4), (2, 8)), jnp.float32),
        "inner_rows": bell_draw(streams_of[1], (GROUPS, OUT_ROWS, D), 1.0, 6.0, ((0, 4), (1, 8)), jnp.float32),
        "inner_norms": bell_draw(streams_of[2], (GROUPS, 3, D), 1.0, 6.0, ((0, 4),), jnp.float32),
        "inner_embed": bell_draw(streams_of[3], (GROUPS, VOCAB, D), 1.0, 6.0, ((0, 4), (1, 8)), jnp.float32),
        "basis": bell_draw(streams_of[4], (D, RANK), D ** -0.5, 0.25, (), jnp.float32),
        "outer_layer": bell_draw(streams_of[5], (N_MP, LAYER_FLAT), 1.0, 6.0, ((0, 8), (1, 32)), jnp.float32),
        "outer_norms": bell_draw(streams_of[6], (3 * D,), 1.0, 6.0, ((0, 32),), jnp.float32),
        "outer_embed": bell_draw(streams_of[7], (N_MP, VOCAB // N_MP, D), 1.0, 6.0, ((0, 8), (1, 32)), jnp.float32),
        "layer_momentum": bell_draw(streams_of[8], (N_MP, LAYER_FLAT), 1.0, 6.0, ((0, 8), (1, 32)), jnp.float32),
        "norm_momentum": bell_draw(streams_of[9], (3 * D,), 1.0, 6.0, ((0, 32),), jnp.float32),
        "embed_momentum": bell_draw(streams_of[10], (N_MP, VOCAB // N_MP, D), 1.0, 6.0, ((0, 8), (1, 32)), jnp.float32),
    }


MU = 0.5
RATE = 0.7


def nesterov(weights, delta, momentum):
    fresh = MU * momentum + delta
    return weights - RATE * (delta + MU * fresh), fresh


def reference(inner_columns, inner_rows, inner_norms, inner_embed, basis, outer_layer, outer_norms, outer_embed, layer_momentum, norm_momentum, embed_momentum):
    count = inner_columns.shape[0]
    col_width = IN_COLS // N_MP
    row_height = OUT_ROWS // N_MP
    blocks_col = inner_columns.reshape(count, D, N_MP, col_width).transpose(0, 2, 1, 3).reshape(count, N_MP, D * col_width)
    blocks_row = inner_rows.reshape(count, N_MP, row_height * D)
    layer_mean = jnp.sum(jnp.concatenate([blocks_col, blocks_row], axis=2), axis=0) / N_GROUP
    norm_mean = jnp.sum(inner_norms.reshape(count, 3 * D), axis=0) / N_GROUP

    def project(rows):
        return jnp.dot(rows, basis, precision=lax.Precision.HIGHEST, preferred_element_type=jnp.float32)

    projected = lax.map(project, inner_embed)
    projected_mean = jnp.sum(projected, axis=0) / N_GROUP
    outer_rows = outer_embed.reshape(VOCAB, D)
    factor = project(outer_rows) - projected_mean
    embed_delta = jnp.dot(factor, basis.T, precision=lax.Precision.HIGHEST, preferred_element_type=jnp.float32)

    new_layer, new_layer_m = nesterov(outer_layer, outer_layer - layer_mean, layer_momentum)
    new_norm, new_norm_m = nesterov(outer_norms, outer_norms - norm_mean, norm_momentum)
    new_rows_embed, new_embed_m = nesterov(outer_rows, embed_delta, embed_momentum.reshape(VOCAB, D))

    split = D * col_width
    new_columns = new_layer[:, :split].reshape(N_MP, D, col_width).transpose(1, 0, 2).reshape(D, IN_COLS)
    new_rows = new_layer[:, split:].reshape(OUT_ROWS, D)
    return (new_columns, new_rows, new_norm.reshape(3, D), new_rows_embed, new_layer_m, new_norm_m, new_embed_m.reshape(N_MP, VOCAB // N_MP, D))
```

```python
import jax
import jax.numpy as jnp
from jax import lax
from jax.experimental import pallas as pl
from jax.experimental.pallas import tpu as pltpu
from jax.sharding import PartitionSpec as P

MU = 0.5
RATE = 0.7
HI = lax.Precision.HIGHEST
AXES = ("group", "dp")

G, Y, L = 4, 4, 2
Z = G * L
PIECES = G * Y * L
FLAT = 13824
RANK = 64
ROWS = 32
WIDTH = 576
NORM = 54
LAYER_TILES = FLAT // 128
FACTOR_TILES = ROWS * RANK // 128
PIECE = 128


def index_of(z, y):
    return (z // L) % G * (Y * L) + y % Y * L + z % L


def moves(step):
    pairs = []
    for z in range(Z):
        for y in range(Y):
            tz, ty = step(z, y)
            pairs.append((index_of(z, y), index_of(tz % Z, ty % Y)))
    return pairs


def swap_one(z, y):
    return (z + 1, y) if z % 2 else (z - 1, y)


def swap_two(z, y):
    return (z + 2, y) if z % 2 else (z - 2, y)


def swap_three(z, y):
    return (z + 3, y) if z % 2 else (z - 3, y)


def shift(dz, dy):
    return moves(lambda z, y: (z + dz, y + dy))


def send(value, pairs):
    return lax.ppermute(value, AXES, pairs)


def place_layer_kernel(where, *refs):
    units, (layer_out, factor_out, norm_out) = refs[:9], refs[9:]
    z0, y0 = where[0], where[1]

    def put(ref, at, zk, yk):
        p = index_of(lax.rem(z0 + zk, Z), lax.rem(y0 + yk, Y))
        layer_out[pl.ds(p * LAYER_TILES, LAYER_TILES), :] = ref[at, pl.ds(FACTOR_TILES, LAYER_TILES), :]
        factor_out[p, :, :] = ref[at, pl.ds(0, FACTOR_TILES), :]
        norm_out[pl.ds(p, 1), :] = ref[at, pl.ds(FACTOR_TILES + LAYER_TILES, 1), :]

    for zk in range(Z):
        for yk in range(Y):
            if zk == Z // 2:
                put(units[4 if yk < 2 else 5], yk % 2, zk, yk)
            else:
                put(units[zk if zk < 4 else zk + 1], yk, zk, yk)


def place_layer(where, units):
    whole = pl.BlockSpec(memory_space=pltpu.VMEM)
    return pl.pallas_call(
        place_layer_kernel,
        out_shape=(
            jax.ShapeDtypeStruct((PIECES * LAYER_TILES, 128), jnp.float32),
            jax.ShapeDtypeStruct((PIECES, FACTOR_TILES, 128), jnp.float32),
            jax.ShapeDtypeStruct((PIECES, 128), jnp.float32),
        ),
        in_specs=[pl.BlockSpec(memory_space=pltpu.SMEM)] + [whole] * 9,
        out_specs=(whole, whole, whole),
        name="place_layer",
    )(where, *units)


def place_embed_kernel(where, own, up, half_low, half_high, down, factor, basis_t, out, rows):
    z0, y0 = where[0], where[1]

    def put(ref, at, zk, yk):
        p = index_of(lax.rem(z0 + zk, Z), lax.rem(y0 + yk, Y))
        rows[pl.ds(pl.multiple_of(p * ROWS, ROWS), ROWS), :] = ref[at]

    for zk in range(Z):
        put(own, zk, zk, 0)
        put(up, zk, zk, 1)
        put(half_low if zk < 4 else half_high, zk % 4, zk, 2)
        put(down, zk, zk, 3)

    for b in range(PIECES * ROWS // 128):
        at = pl.ds(b * 128, 128)
        delta = jnp.dot(factor[at, :], basis_t[...], precision=HI, preferred_element_type=jnp.float32)
        out[:, at] = (rows[at, :] - (RATE * (1 + MU)) * delta).T


def place_embed(where, own, up, half_low, half_high, down, factor, basis_t):
    whole = pl.BlockSpec(memory_space=pltpu.VMEM)
    return pl.pallas_call(
        place_embed_kernel,
        out_shape=jax.ShapeDtypeStruct((WIDTH, PIECES * ROWS), jnp.float32),
        in_specs=[pl.BlockSpec(memory_space=pltpu.SMEM)] + [whole] * 7,
        out_specs=whole,
        scratch_shapes=[pltpu.VMEM((PIECES * ROWS, WIDTH), jnp.float32)],
        name="place_embed",
    )(where, own, up, half_low, half_high, down, factor, basis_t)


def local(
    inner_columns,
    inner_rows,
    inner_norms,
    inner_embed,
    basis,
    outer_layer,
    outer_norms,
    outer_embed,
    layer_momentum,
    norm_momentum,
    embed_momentum,
):
    group, place = lax.axis_index("group"), lax.axis_index("dp")
    y0, side = place // L, place % L
    z0 = group * L + side
    where = jnp.stack([z0, y0]).astype(jnp.int32)
    outer_rows = outer_embed[0]

    kept = outer_rows - (RATE * MU * MU) * embed_momentum[0]
    ups, downs = [], []
    up = down = kept
    for k in range(1, Z // 2):
        up, down = send(up, shift(-1, 0)), send(down, shift(1, 0))
        ups.append(up)
        downs.append(down)
    half = ROWS // 2
    far = jnp.concatenate([send(up[:half], shift(-1, 0)), send(down[half:], shift(1, 0))], 0)
    embed_own = jnp.stack([kept, *ups, far, *downs[::-1]])
    embed_up, embed_down = send(embed_own, shift(0, -1)), send(embed_own, shift(0, 1))
    embed_low = send(embed_up[: Z // 2], shift(0, -1))
    embed_high = send(embed_down[Z // 2 :], shift(0, 1))

    flat = jnp.concatenate([inner_columns[0].reshape(-1), inner_rows[0].reshape(-1)])
    norms = inner_norms[0].reshape(-1)
    projected = jnp.dot(inner_embed[0], basis, precision=HI, preferred_element_type=jnp.float32)

    def piece(z):
        p = index_of(z % Z, y0)
        return jnp.concatenate(
            [
                lax.dynamic_slice(projected, (p * ROWS, 0), (ROWS, RANK)).reshape(-1),
                lax.dynamic_slice(flat, (p * FLAT,), (FLAT,)),
                lax.dynamic_slice(norms, (p * NORM,), (NORM,)),
            ]
        )

    away = 2 * side - 1
    total = piece(z0)
    for k, step in ((1, swap_one), (2, swap_two), (3, swap_three)):
        total = total + send(piece(z0 + k * away + Z), moves(step))
    mean = total / G
    split = ROWS * RANK
    factor = (
        jnp.dot(outer_rows, basis, precision=HI, preferred_element_type=jnp.float32)
        - mean[:split].reshape(ROWS, RANK)
    )

    def nesterov(weights, delta, momentum):
        fresh = MU * momentum + delta
        return weights - RATE * (delta + MU * fresh), fresh

    new_layer, new_layer_m = nesterov(
        outer_layer[0], outer_layer[0] - mean[split : split + FLAT], layer_momentum[0]
    )
    new_norm, new_norm_m = nesterov(outer_norms, outer_norms - mean[split + FLAT :], norm_momentum)
    new_embed_m = MU * embed_momentum[0] + jnp.dot(
        factor, basis.T, precision=HI, preferred_element_type=jnp.float32
    )

    own = jnp.concatenate([factor.reshape(-1), new_layer, new_norm])
    own = jnp.pad(own, (0, PIECE * 128 - own.shape[0])).reshape(PIECE, 128)

    y_up, y_down = send(own, shift(0, -1)), send(own, shift(0, 1))
    half = PIECE // 2
    y_far = jnp.concatenate([send(y_up[:half], shift(0, -1)), send(y_down[half:], shift(0, 1))], 0)
    unit = jnp.stack([own, y_up, y_far, y_down])
    ups, downs = [], []
    up = down = unit
    for k in range(1, Z // 2):
        up, down = send(up, shift(-1, 0)), send(down, shift(1, 0))
        ups.append(up)
        downs.append(down)
    low, high = send(up[: Y // 2], shift(-1, 0)), send(down[Y // 2 :], shift(1, 0))
    layer_all, factor_all, norm_all = place_layer(where, (unit, *ups, low, high, *downs[::-1]))
    layer_whole = layer_all.reshape(-1)
    columns = inner_columns.shape[1] * inner_columns.shape[2]
    new_columns = layer_whole[:columns].reshape(inner_columns.shape[1:])
    new_rows = layer_whole[columns:].reshape(inner_rows.shape[1:])
    new_norms = norm_all[:, :NORM].reshape(3, WIDTH)
    new_embed = place_embed(
        where,
        embed_own,
        embed_up,
        embed_low,
        embed_high,
        embed_down,
        factor_all.reshape(PIECES * ROWS, RANK),
        basis.T,
    ).T
    return (
        new_columns,
        new_rows,
        new_norms,
        new_embed,
        new_layer_m[None, :],
        new_norm_m,
        new_embed_m[None, :, :],
    )


def solution(mesh):
    in_specs = (
        P("group", None, "mp"),
        P("group", "mp", None),
        P("group", None, None),
        P("group", "mp", None),
        P(),
        P("mp", AXES),
        P(AXES),
        P("mp", AXES, None),
        P("mp", AXES),
        P(AXES),
        P("mp", AXES, None),
    )
    out_specs = (
        P(None, "mp"),
        P("mp", None),
        P(),
        P("mp", None),
        P("mp", AXES),
        P(AXES),
        P("mp", AXES, None),
    )
    return jax.shard_map(local, mesh=mesh, in_specs=in_specs, out_specs=out_specs, check_vma=False)
```

```python
import jax
import jax.numpy as jnp
from jax import lax
from jax.experimental import pallas as pl
from jax.experimental.pallas import tpu as pltpu
from jax.sharding import PartitionSpec as P

MU = 0.5
RATE = 0.7
HI = lax.Precision.HIGHEST
AXES = ("group", "dp")

G, Y, L = 4, 4, 2
Z = G * L
PIECES = G * Y * L
FLAT = 13824
RANK = 64
ROWS = 32
WIDTH = 576
NORM = 54
LAYER_TILES = FLAT // 128
FACTOR_TILES = ROWS * RANK // 128
PIECE = 128
NORM_AT = FACTOR_TILES + LAYER_TILES
MESSAGE = 144
COL_WIDTH = 504
ROW_HEIGHT = 264
COL_TILES = WIDTH * COL_WIDTH // 128


def index_of(z, y):
    return (z // L) % G * (Y * L) + y % Y * L + z % L


def moves(step):
    pairs = []
    for z in range(Z):
        for y in range(Y):
            tz, ty = step(z, y)
            pairs.append((index_of(z, y), index_of(tz % Z, ty % Y)))
    return pairs


def swap_one(z, y):
    return (z + 1, y) if z % 2 else (z - 1, y)


def swap_two(z, y):
    return (z + 2, y) if z % 2 else (z - 2, y)


def swap_three(z, y):
    return (z + 3, y) if z % 2 else (z - 3, y)


def shift(dz, dy):
    return moves(lambda z, y: (z + dz, y + dy))


def send(value, pairs):
    return lax.ppermute(value, AXES, pairs)


def segments(start, width):
    found, at = [], 0
    while at < 128:
        row, column = divmod(start + at, width)
        tile, lane = divmod(column, 128)
        count = min(128 - at, 128 - lane, width - column)
        found.append((row, tile, lane, at, count))
        at += count
    return found


def join(parts):
    out = None
    for value, lane, at, count in parts:
        turn = (at - lane) % 128
        value = pltpu.roll(value, turn, 1) if turn else value
        if out is None:
            out = value
        else:
            lanes = lax.broadcasted_iota(jnp.int32, value.shape, 1)
            out = jnp.where(lanes >= at, value, out)
    return out


def flatten(tiles, flat, base, width, period, groups):
    made = period * width // 128
    for j in range(made):
        flat[pl.ds(base + j, groups, stride=made), :] = join(
            [
                (tiles[tile, pl.ds(row, groups, stride=period), :], lane, at, count)
                for row, tile, lane, at, count in segments(128 * j, width)
            ]
        )


def unflatten(flat, base, tiles, width, period, groups):
    made = period * width // 128
    for row in range(period):
        for tile in range((width + 127) // 128):
            start = row * width + tile * 128
            line, lane = divmod(start, 128)
            count = min(128, width - tile * 128)
            parts = [(flat[pl.ds(base + line, groups, stride=made), :], lane, 0, 128 - lane)]
            if 128 - lane < count:
                parts.append((flat[pl.ds(base + line + 1, groups, stride=made), :], 0, 128 - lane, lane))
            tiles[tile, pl.ds(row, groups, stride=period), :] = join(parts)


def to_tiles(rows, tiles):
    width = rows.shape[1]
    for tile in range(tiles.shape[0]):
        count = min(128, width - tile * 128)
        tiles[tile, pl.ds(0, rows.shape[0]), pl.ds(0, count)] = rows[:, pl.ds(tile * 128, count)]


def from_tiles(tiles, rows):
    width = rows.shape[1]
    for tile in range(tiles.shape[0]):
        count = min(128, width - tile * 128)
        rows[:, pl.ds(tile * 128, count)] = tiles[tile, pl.ds(0, rows.shape[0]), pl.ds(0, count)]


def pack_kernel(where, columns, rows, norms, embed_t, basis_t, *refs):
    messages = refs[:4]
    cbuf, rbuf, ebuf, ctiles, rtiles, flat, sem = refs[4:]
    z0, y0 = where[0], where[1]
    away = 2 * lax.rem(z0, L) - 1
    pieces = [index_of(lax.rem(z0 + k * away + Z, Z), y0) for k in range(G)]
    copies = [pltpu.make_async_copy(columns, cbuf, sem.at[0]), pltpu.make_async_copy(rows, rbuf, sem.at[1])]
    for k, p in enumerate(pieces):
        at = pl.ds(pl.multiple_of(p // 4 * 128, 128), 128)
        copies.append(pltpu.make_async_copy(embed_t.at[:, at], ebuf.at[k], sem.at[2 + k]))
    for copy in copies:
        copy.start()
    copies[0].wait()
    to_tiles(cbuf, ctiles)
    flatten(ctiles, flat, 0, COL_WIDTH, 16, WIDTH // 16)
    copies[1].wait()
    to_tiles(rbuf, rtiles)
    flatten(rtiles, flat, COL_TILES, WIDTH, 2, ROW_HEIGHT // 2)
    for copy in copies[2:]:
        copy.wait()
    picked = None
    lanes = lax.broadcasted_iota(jnp.int32, (WIDTH, 128), 1)
    for k, p in enumerate(pieces):
        turned = pltpu.roll(ebuf[k], lax.rem(k * ROWS + 128 - lax.rem(p, 4) * ROWS, 128), 1)
        picked = turned if picked is None else jnp.where(lanes >= k * ROWS, turned, picked)
    projected = jnp.dot(basis_t[...], picked, precision=HI, preferred_element_type=jnp.float32).T
    for k, (p, message) in enumerate(zip(pieces, messages)):
        message[pl.ds(0, FACTOR_TILES), :] = jnp.concatenate(
            [projected[k * ROWS : k * ROWS + 16], projected[k * ROWS + 16 : (k + 1) * ROWS]], 1
        )
        message[pl.ds(FACTOR_TILES, LAYER_TILES), :] = flat[pl.ds(p * LAYER_TILES, LAYER_TILES), :]
        message[pl.ds(NORM_AT, MESSAGE - NORM_AT), :] = jnp.zeros((MESSAGE - NORM_AT, 128), jnp.float32)
        for row in range(3):
            for tile in range(5):
                count = min(128, WIDTH - tile * 128)
                message[pl.ds(NORM_AT + row * 5 + tile, 1), pl.ds(0, count)] = norms[
                    pl.ds(row, 1), pl.ds(tile * 128, count)
                ]


VMEM = pl.BlockSpec(memory_space=pltpu.VMEM)
SMEM = pl.BlockSpec(memory_space=pltpu.SMEM)
ANY = pl.BlockSpec(memory_space=pl.ANY)


def f32(*shape):
    return jax.ShapeDtypeStruct(shape, jnp.float32)


def pack(where, columns, rows, norms, embed_t, basis_t):
    return pl.pallas_call(
        pack_kernel,
        out_shape=(f32(MESSAGE, 128),) * 4,
        in_specs=[SMEM, ANY, ANY, VMEM, ANY, VMEM],
        out_specs=(VMEM,) * 4,
        scratch_shapes=[
            pltpu.VMEM(columns.shape, jnp.float32),
            pltpu.VMEM(rows.shape, jnp.float32),
            pltpu.VMEM((G, WIDTH, 128), jnp.float32),
            pltpu.VMEM((4, 640, 128), jnp.float32),
            pltpu.VMEM((5, 272, 128), jnp.float32),
            pltpu.VMEM((3496, 128), jnp.float32),
            pltpu.SemaphoreType.DMA((6,)),
        ],
        name="pack",
    )(where, columns, rows, norms, embed_t, basis_t)


def update_kernel(own, one, two, three, weights, momentum, base, norm_part, piece, fresh_out, factor_out, mean_out):
    mean = (own[...] + one[...] + two[...] + three[...]) * (1 / G)
    factor = base[...] - mean[:FACTOR_TILES]
    delta = weights[...] - mean[FACTOR_TILES:NORM_AT]
    fresh = MU * momentum[...] + delta
    piece[pl.ds(0, FACTOR_TILES), :] = factor
    piece[pl.ds(FACTOR_TILES, LAYER_TILES), :] = weights[...] - RATE * (delta + MU * fresh)
    piece[pl.ds(NORM_AT, PIECE - NORM_AT), :] = jnp.zeros((PIECE - NORM_AT, 128), jnp.float32)
    piece[pl.ds(NORM_AT, 1), :] = norm_part[...]
    fresh_out[...] = fresh
    factor_out[...] = factor
    mean_out[...] = mean[NORM_AT:]


def update(*args):
    return pl.pallas_call(
        update_kernel,
        out_shape=(
            f32(PIECE, 128),
            f32(LAYER_TILES, 128),
            f32(FACTOR_TILES, 128),
            f32(MESSAGE - NORM_AT, 128),
        ),
        in_specs=[VMEM] * 8,
        out_specs=(VMEM,) * 4,
        name="update",
    )(*args)


def place_embed_kernel(where, own, up, half_low, half_high, down, out, rows):
    z0, y0 = where[0], where[1]

    def put(ref, at, zk, yk):
        p = index_of(lax.rem(z0 + zk, Z), lax.rem(y0 + yk, Y))
        rows[pl.ds(pl.multiple_of(p * ROWS, ROWS), ROWS), :] = ref[at]

    for zk in range(Z):
        put(own, zk, zk, 0)
        put(up, zk, zk, 1)
        put(half_low if zk < 4 else half_high, zk % 4, zk, 2)
        put(down, zk, zk, 3)
    for b in range(PIECES * ROWS // 128):
        at = pl.ds(b * 128, 128)
        out[:, at] = rows[at, :].T


def place_embed(where, *units):
    return pl.pallas_call(
        place_embed_kernel,
        out_shape=f32(WIDTH, PIECES * ROWS),
        in_specs=[SMEM] + [VMEM] * 5,
        out_specs=VMEM,
        scratch_shapes=[pltpu.VMEM((PIECES * ROWS, WIDTH), jnp.float32)],
        name="place_embed",
    )(where, *units)


def split(value):
    high = value.astype(jnp.bfloat16)
    return high, (value - high.astype(jnp.float32)).astype(jnp.bfloat16)


def finish_kernel(where, *refs):
    units, (rest, basis, mean) = refs[:9], refs[9:12]
    columns_out, rows_out, norms_out, embed_out = refs[12:16]
    flat, factor, norm, ctiles, rtiles, cbuf, rbuf, ebuf, sem = refs[16:]
    z0, y0 = where[0], where[1]

    def put(ref, at, zk, yk):
        p = index_of(lax.rem(z0 + zk, Z), lax.rem(y0 + yk, Y))
        flat[pl.ds(p * LAYER_TILES, LAYER_TILES), :] = ref[at, pl.ds(FACTOR_TILES, LAYER_TILES), :]
        packed = ref[at, pl.ds(0, FACTOR_TILES), :]
        factor[pl.ds(pl.multiple_of(p * ROWS, ROWS), ROWS), :] = jnp.concatenate(
            [packed[:, :RANK], packed[:, RANK:]], 0
        )
        norm[pl.ds(p, 1), :] = ref[at, pl.ds(NORM_AT, 1), :]

    for zk in range(Z):
        for yk in range(Y):
            if zk == Z // 2:
                put(units[4 if yk < 2 else 5], yk % 2, zk, yk)
            else:
                put(units[zk if zk < 4 else zk + 1], yk, zk, yk)

    high, low = split(factor[...])
    right = jnp.concatenate([high, high, low, low], 1)
    high, low = split(basis[...] * (RATE * (1 + MU)))
    left = jnp.concatenate([high, low, high, low], 1)
    ebuf[...] = rest[...] - lax.dot_general(
        left, right, (((1,), (1,)), ((), ())), preferred_element_type=jnp.float32
    )
    embed_copy = pltpu.make_async_copy(ebuf, embed_out, sem.at[0])
    embed_copy.start()
    unflatten(flat, 0, ctiles, COL_WIDTH, 16, WIDTH // 16)
    from_tiles(ctiles, cbuf)
    columns_copy = pltpu.make_async_copy(cbuf, columns_out, sem.at[1])
    columns_copy.start()
    unflatten(flat, COL_TILES, rtiles, WIDTH, 2, ROW_HEIGHT // 2)
    from_tiles(rtiles, rbuf)
    rows_copy = pltpu.make_async_copy(rbuf, rows_out, sem.at[2])
    rows_copy.start()
    for row in range(3):
        for tile in range(5):
            start, count = row * WIDTH + tile * 128, min(128, WIDTH - tile * 128)
            parts, at = [], 0
            while at < count:
                p, lane = divmod(start + at, NORM)
                size = min(count - at, NORM - lane)
                parts.append((norm[pl.ds(p, 1), :], lane, at, size))
                at += size
            value = join(parts) + (RATE * (1 + MU)) * mean[pl.ds(row * 5 + tile, 1), :]
            norms_out[pl.ds(row, 1), pl.ds(tile * 128, count)] = value[:, :count]
    embed_copy.wait()
    columns_copy.wait()
    rows_copy.wait()


def finish(where, units, rest, basis, mean):
    return pl.pallas_call(
        finish_kernel,
        out_shape=(
            f32(WIDTH, COL_WIDTH),
            f32(ROW_HEIGHT, WIDTH),
            f32(3, WIDTH),
            f32(WIDTH, PIECES * ROWS),
        ),
        in_specs=[SMEM] + [VMEM] * 12,
        out_specs=(ANY, ANY, VMEM, ANY),
        scratch_shapes=[
            pltpu.VMEM((3496, 128), jnp.float32),
            pltpu.VMEM((PIECES * ROWS, RANK), jnp.float32),
            pltpu.VMEM((PIECES, 128), jnp.float32),
            pltpu.VMEM((4, 640, 128), jnp.float32),
            pltpu.VMEM((5, 272, 128), jnp.float32),
            pltpu.VMEM((WIDTH, COL_WIDTH), jnp.float32),
            pltpu.VMEM((ROW_HEIGHT, WIDTH), jnp.float32),
            pltpu.VMEM((WIDTH, PIECES * ROWS), jnp.float32),
            pltpu.SemaphoreType.DMA((3,)),
        ],
        name="finish",
    )(where, *units, rest, basis, mean)


def local(
    inner_columns,
    inner_rows,
    inner_norms,
    inner_embed,
    basis,
    outer_layer,
    outer_norms,
    outer_embed,
    layer_momentum,
    norm_momentum,
    embed_momentum,
):
    group, place = lax.axis_index("group"), lax.axis_index("dp")
    y0, side = place // L, place % L
    z0 = group * L + side
    where = jnp.stack([z0, y0]).astype(jnp.int32)
    outer_rows = outer_embed[0]

    kept = outer_rows - (RATE * MU * MU) * embed_momentum[0]
    ups, downs = [], []
    up = down = kept
    for k in range(1, Z // 2):
        up, down = send(up, shift(-1, 0)), send(down, shift(1, 0))
        ups.append(up)
        downs.append(down)
    half = ROWS // 2
    far = jnp.concatenate([send(up[:half], shift(-1, 0)), send(down[half:], shift(1, 0))], 0)
    embed_own = jnp.stack([kept, *ups, far, *downs[::-1]])
    embed_up, embed_down = send(embed_own, shift(0, -1)), send(embed_own, shift(0, 1))
    embed_low = send(embed_up[: Z // 2], shift(0, -1))
    embed_high = send(embed_down[Z // 2 :], shift(0, 1))

    own, *away = pack(where, inner_columns[0], inner_rows[0], inner_norms[0], inner_embed[0].T, basis.T)
    came = [send(m, moves(step)) for m, step in zip(away, (swap_one, swap_two, swap_three))]
    base = jnp.dot(outer_rows, basis, precision=HI, preferred_element_type=jnp.float32)
    base = jnp.concatenate([base[: ROWS // 2], base[ROWS // 2 :]], 1)
    norm_part = outer_norms - RATE * ((1 + MU) * outer_norms + MU * MU * norm_momentum)
    own, new_layer_m, factor, mean = update(
        own,
        *came,
        outer_layer.reshape(LAYER_TILES, 128),
        layer_momentum.reshape(LAYER_TILES, 128),
        base,
        jnp.pad(norm_part, (0, 128 - NORM))[None],
    )
    factor = jnp.concatenate([factor[:, :RANK], factor[:, RANK:]], 0)
    new_embed_m = MU * embed_momentum[0] + jnp.dot(
        factor, basis.T, precision=HI, preferred_element_type=jnp.float32
    )
    norm_mean = mean[:15].reshape(3, 640)[:, :WIDTH].reshape(-1)
    mine = lax.dynamic_slice(norm_mean, (index_of(z0, y0) * NORM,), (NORM,))
    new_norm_m = MU * norm_momentum + (outer_norms - mine)

    y_up, y_down = send(own, shift(0, -1)), send(own, shift(0, 1))
    half = PIECE // 2
    y_far = jnp.concatenate([send(y_up[:half], shift(0, -1)), send(y_down[half:], shift(0, 1))], 0)
    unit = jnp.stack([own, y_up, y_far, y_down])
    ups, downs = [], []
    up = down = unit
    for k in range(1, Z // 2):
        up, down = send(up, shift(-1, 0)), send(down, shift(1, 0))
        ups.append(up)
        downs.append(down)
    low, high = send(up[: Y // 2], shift(-1, 0)), send(down[Y // 2 :], shift(1, 0))
    rest = place_embed(where, embed_own, embed_up, embed_low, embed_high, embed_down)
    new_columns, new_rows, new_norms, new_embed = finish(
        where, (unit, *ups, low, high, *downs[::-1]), rest, basis, mean
    )
    return (
        new_columns,
        new_rows,
        new_norms,
        new_embed.T,
        new_layer_m.reshape(1, -1),
        new_norm_m,
        new_embed_m[None, :, :],
    )


def solution(mesh):
    in_specs = (
        P("group", None, "mp"),
        P("group", "mp", None),
        P("group", None, None),
        P("group", "mp", None),
        P(),
        P("mp", AXES),
        P(AXES),
        P("mp", AXES, None),
        P("mp", AXES),
        P(AXES),
        P("mp", AXES, None),
    )
    out_specs = (
        P(None, "mp"),
        P("mp", None),
        P(),
        P("mp", None),
        P("mp", AXES),
        P(AXES),
        P("mp", AXES, None),
    )
    return jax.shard_map(local, mesh=mesh, in_specs=in_specs, out_specs=out_specs, check_vma=False)
```

```python
import jax
import jax.numpy as jnp
from jax import lax
from jax.experimental import pallas as pl
from jax.experimental.pallas import tpu as pltpu
from jax.sharding import PartitionSpec as P

MU = 0.5
RATE = 0.7
HI = lax.Precision.HIGHEST
AXES = ("group", "dp")

G, Y, L = 4, 4, 2
Z = G * L
PIECES = G * Y * L
FLAT = 13824
RANK = 64
ROWS = 32
WIDTH = 576
NORM = 54
LAYER_TILES = FLAT // 128
FACTOR_TILES = ROWS * RANK // 128
PIECE = 128
NORM_AT = FACTOR_TILES + LAYER_TILES
MESSAGE = 144
COL_WIDTH = 504
ROW_HEIGHT = 264
COL_TILES = WIDTH * COL_WIDTH // 128


def index_of(z, y):
    return (z // L) % G * (Y * L) + y % Y * L + z % L


def position():
    place = lax.axis_index("dp")
    return lax.axis_index("group") * L + lax.rem(place, L), place // L


def moves(step):
    pairs = []
    for z in range(Z):
        for y in range(Y):
            tz, ty = step(z, y)
            pairs.append((index_of(z, y), index_of(tz % Z, ty % Y)))
    return pairs


def swap_one(z, y):
    return (z + 1, y) if z % 2 else (z - 1, y)


def swap_two(z, y):
    return (z + 2, y) if z % 2 else (z - 2, y)


def swap_three(z, y):
    return (z + 3, y) if z % 2 else (z - 3, y)


def shift(dz, dy):
    return moves(lambda z, y: (z + dz, y + dy))


def send(value, pairs):
    return lax.ppermute(value, AXES, pairs)


def segments(start, width):
    found, at = [], 0
    while at < 128:
        row, column = divmod(start + at, width)
        tile, lane = divmod(column, 128)
        count = min(128 - at, 128 - lane, width - column)
        found.append((row, tile, lane, at, count))
        at += count
    return found


def join(parts):
    out = None
    for value, lane, at, count in parts:
        turn = (at - lane) % 128
        value = pltpu.roll(value, turn, 1) if turn else value
        if out is None:
            out = value
        else:
            lanes = lax.broadcasted_iota(jnp.int32, value.shape, 1)
            out = jnp.where(lanes >= at, value, out)
    return out


def flatten(tiles, flat, base, width, period, groups):
    made = period * width // 128
    for j in range(made):
        flat[pl.ds(base + j, groups, stride=made), :] = join(
            [
                (tiles[tile, pl.ds(row, groups, stride=period), :], lane, at, count)
                for row, tile, lane, at, count in segments(128 * j, width)
            ]
        )


def unflatten(flat, base, tiles, width, period, groups):
    made = period * width // 128
    for row in range(period):
        for tile in range((width + 127) // 128):
            start = row * width + tile * 128
            line, lane = divmod(start, 128)
            count = min(128, width - tile * 128)
            parts = [(flat[pl.ds(base + line, groups, stride=made), :], lane, 0, 128 - lane)]
            if 128 - lane < count:
                parts.append((flat[pl.ds(base + line + 1, groups, stride=made), :], 0, 128 - lane, lane))
            tiles[tile, pl.ds(row, groups, stride=period), :] = join(parts)


def to_tiles(rows, tiles):
    width = rows.shape[1]
    for tile in range(tiles.shape[0]):
        count = min(128, width - tile * 128)
        tiles[tile, pl.ds(0, rows.shape[0]), pl.ds(0, count)] = rows[:, pl.ds(tile * 128, count)]


def from_tiles(tiles, rows):
    width = rows.shape[1]
    for tile in range(tiles.shape[0]):
        count = min(128, width - tile * 128)
        rows[:, pl.ds(tile * 128, count)] = tiles[tile, pl.ds(0, rows.shape[0]), pl.ds(0, count)]


def pack_kernel(columns, rows, norms, embed_t, basis_t, *refs):
    messages = refs[:4]
    cbuf, rbuf, ebuf, ctiles, rtiles, flat, sem = refs[4:]
    z0, y0 = position()
    away = 2 * lax.rem(z0, L) - 1
    pieces = [index_of(lax.rem(z0 + k * away + Z, Z), y0) for k in range(G)]
    copies = [pltpu.make_async_copy(columns, cbuf, sem.at[0]), pltpu.make_async_copy(rows, rbuf, sem.at[1])]
    for k, p in enumerate(pieces):
        at = pl.ds(pl.multiple_of(p // 4 * 128, 128), 128)
        copies.append(pltpu.make_async_copy(embed_t.at[:, at], ebuf.at[k], sem.at[2 + k]))
    for copy in copies:
        copy.start()
    copies[0].wait()
    to_tiles(cbuf, ctiles)
    flatten(ctiles, flat, 0, COL_WIDTH, 16, WIDTH // 16)
    copies[1].wait()
    to_tiles(rbuf, rtiles)
    flatten(rtiles, flat, COL_TILES, WIDTH, 2, ROW_HEIGHT // 2)
    for copy in copies[2:]:
        copy.wait()
    picked = None
    lanes = lax.broadcasted_iota(jnp.int32, (WIDTH, 128), 1)
    for k, p in enumerate(pieces):
        turned = pltpu.roll(ebuf[k], lax.rem(k * ROWS + 128 - lax.rem(p, 4) * ROWS, 128), 1)
        picked = turned if picked is None else jnp.where(lanes >= k * ROWS, turned, picked)
    projected = jnp.dot(basis_t[...], picked, precision=HI, preferred_element_type=jnp.float32).T
    for k, (p, message) in enumerate(zip(pieces, messages)):
        message[pl.ds(0, FACTOR_TILES), :] = jnp.concatenate(
            [projected[k * ROWS : k * ROWS + 16], projected[k * ROWS + 16 : (k + 1) * ROWS]], 1
        )
        message[pl.ds(FACTOR_TILES, LAYER_TILES), :] = flat[pl.ds(p * LAYER_TILES, LAYER_TILES), :]
        message[pl.ds(NORM_AT, MESSAGE - NORM_AT), :] = jnp.zeros((MESSAGE - NORM_AT, 128), jnp.float32)
        for row in range(3):
            for tile in range(5):
                count = min(128, WIDTH - tile * 128)
                message[pl.ds(NORM_AT + row * 5 + tile, 1), pl.ds(0, count)] = norms[
                    row, :, pl.ds(tile * 128, count)
                ]


VMEM = pl.BlockSpec(memory_space=pltpu.VMEM)
ANY = pl.BlockSpec(memory_space=pl.ANY)


def f32(*shape):
    return jax.ShapeDtypeStruct(shape, jnp.float32)


def pack(columns, rows, norms, embed_t, basis_t):
    return pl.pallas_call(
        pack_kernel,
        out_shape=(f32(MESSAGE, 128),) * 4,
        in_specs=[ANY, ANY, VMEM, ANY, VMEM],
        out_specs=(VMEM,) * 4,
        scratch_shapes=[
            pltpu.VMEM(columns.shape, jnp.float32),
            pltpu.VMEM(rows.shape, jnp.float32),
            pltpu.VMEM((G, WIDTH, 128), jnp.float32),
            pltpu.VMEM((4, 640, 128), jnp.float32),
            pltpu.VMEM((5, 272, 128), jnp.float32),
            pltpu.VMEM((3496, 128), jnp.float32),
            pltpu.SemaphoreType.DMA((6,)),
        ],
        compiler_params=pltpu.CompilerParams(vmem_limit_bytes=60 << 20),
        name="pack",
    )(columns, rows, norms, embed_t, basis_t)


def update_kernel(own, one, two, three, weights, momentum, base, norm_part, piece, fresh_out, factor_out, mean_out):
    mean = (own[...] + one[...] + two[...] + three[...]) * (1 / G)
    factor = base[...] - mean[:FACTOR_TILES]
    delta = weights[...] - mean[FACTOR_TILES:NORM_AT]
    fresh = MU * momentum[...] + delta
    piece[pl.ds(0, FACTOR_TILES), :] = factor
    piece[pl.ds(FACTOR_TILES, LAYER_TILES), :] = weights[...] - RATE * (delta + MU * fresh)
    piece[pl.ds(NORM_AT, PIECE - NORM_AT), :] = jnp.zeros((PIECE - NORM_AT, 128), jnp.float32)
    piece[pl.ds(NORM_AT, 1), :] = norm_part[...]
    fresh_out[...] = fresh
    factor_out[...] = factor
    mean_out[...] = mean[NORM_AT:]


def update(*args):
    return pl.pallas_call(
        update_kernel,
        out_shape=(
            f32(PIECE, 128),
            f32(LAYER_TILES, 128),
            f32(FACTOR_TILES, 128),
            f32(MESSAGE - NORM_AT, 128),
        ),
        in_specs=[VMEM] * 8,
        out_specs=(VMEM,) * 4,
        compiler_params=pltpu.CompilerParams(vmem_limit_bytes=3 << 20),
        name="update",
    )(*args)


def place_embed_kernel(own, up, half_low, half_high, down, out, rows):
    z0, y0 = position()

    def put(ref, at, zk, yk):
        p = index_of(lax.rem(z0 + zk, Z), lax.rem(y0 + yk, Y))
        rows[pl.ds(pl.multiple_of(p * ROWS, ROWS), ROWS), :] = ref[at]

    for zk in range(Z):
        put(own, zk, zk, 0)
        put(up, zk, zk, 1)
        put(half_low if zk < 4 else half_high, zk % 4, zk, 2)
        put(down, zk, zk, 3)
    for b in range(PIECES * ROWS // 128):
        at = pl.ds(b * 128, 128)
        out[:, at] = rows[at, :].T


def place_embed(*units):
    return pl.pallas_call(
        place_embed_kernel,
        out_shape=f32(WIDTH, PIECES * ROWS),
        in_specs=[VMEM] * 5,
        out_specs=VMEM,
        scratch_shapes=[pltpu.VMEM((PIECES * ROWS, WIDTH), jnp.float32)],
        compiler_params=pltpu.CompilerParams(vmem_limit_bytes=12 << 20),
        name="place_embed",
    )(*units)


def split(value):
    high = value.astype(jnp.bfloat16)
    return high, (value - high.astype(jnp.float32)).astype(jnp.bfloat16)


def finish_kernel(*refs):
    units, (rest, basis, mean) = refs[:9], refs[9:12]
    columns_out, rows_out, norms_out, embed_out = refs[12:16]
    flat, factor, norm, ctiles, rtiles, cbuf, rbuf, ebuf, sem = refs[16:]
    z0, y0 = position()

    def put(ref, at, zk, yk):
        p = index_of(lax.rem(z0 + zk, Z), lax.rem(y0 + yk, Y))
        flat[pl.ds(p * LAYER_TILES, LAYER_TILES), :] = ref[at, pl.ds(FACTOR_TILES, LAYER_TILES), :]
        packed = ref[at, pl.ds(0, FACTOR_TILES), :]
        factor[pl.ds(pl.multiple_of(p * ROWS, ROWS), ROWS), :] = jnp.concatenate(
            [packed[:, :RANK], packed[:, RANK:]], 0
        )
        norm[pl.ds(p, 1), :] = ref[at, pl.ds(NORM_AT, 1), :]

    for zk in range(Z):
        for yk in range(Y):
            if zk == Z // 2:
                put(units[4 if yk < 2 else 5], yk % 2, zk, yk)
            else:
                put(units[zk if zk < 4 else zk + 1], yk, zk, yk)

    high, low = split(factor[...])
    right = jnp.concatenate([high, high, low, low], 1)
    high, low = split(basis[...] * (RATE * (1 + MU)))
    left = jnp.concatenate([high, low, high, low], 1)
    ebuf[...] = rest[...] - lax.dot_general(
        left, right, (((1,), (1,)), ((), ())), preferred_element_type=jnp.float32
    )
    embed_copy = pltpu.make_async_copy(ebuf, embed_out, sem.at[0])
    embed_copy.start()
    unflatten(flat, 0, ctiles, COL_WIDTH, 16, WIDTH // 16)
    from_tiles(ctiles, cbuf)
    columns_copy = pltpu.make_async_copy(cbuf, columns_out, sem.at[1])
    columns_copy.start()
    unflatten(flat, COL_TILES, rtiles, WIDTH, 2, ROW_HEIGHT // 2)
    from_tiles(rtiles, rbuf)
    rows_copy = pltpu.make_async_copy(rbuf, rows_out, sem.at[2])
    rows_copy.start()
    for row in range(3):
        for tile in range(5):
            start, count = row * WIDTH + tile * 128, min(128, WIDTH - tile * 128)
            parts, at = [], 0
            while at < count:
                p, lane = divmod(start + at, NORM)
                size = min(count - at, NORM - lane)
                parts.append((norm[pl.ds(p, 1), :], lane, at, size))
                at += size
            value = join(parts) + (RATE * (1 + MU)) * mean[pl.ds(row * 5 + tile, 1), :]
            norms_out[pl.ds(row, 1), pl.ds(tile * 128, count)] = value[:, :count]
    embed_copy.wait()
    columns_copy.wait()
    rows_copy.wait()


def finish(units, rest, basis, mean):
    return pl.pallas_call(
        finish_kernel,
        out_shape=(
            f32(WIDTH, COL_WIDTH),
            f32(ROW_HEIGHT, WIDTH),
            f32(3, WIDTH),
            f32(WIDTH, PIECES * ROWS),
        ),
        in_specs=[VMEM] * 12,
        out_specs=(ANY, ANY, VMEM, ANY),
        scratch_shapes=[
            pltpu.VMEM((3496, 128), jnp.float32),
            pltpu.VMEM((PIECES * ROWS, RANK), jnp.float32),
            pltpu.VMEM((PIECES, 128), jnp.float32),
            pltpu.VMEM((4, 640, 128), jnp.float32),
            pltpu.VMEM((5, 272, 128), jnp.float32),
            pltpu.VMEM((WIDTH, COL_WIDTH), jnp.float32),
            pltpu.VMEM((ROW_HEIGHT, WIDTH), jnp.float32),
            pltpu.VMEM((WIDTH, PIECES * ROWS), jnp.float32),
            pltpu.SemaphoreType.DMA((3,)),
        ],
        compiler_params=pltpu.CompilerParams(vmem_limit_bytes=18 << 20),
        name="finish",
    )(*units, rest, basis, mean)


def local(
    inner_columns,
    inner_rows,
    inner_norms,
    inner_embed,
    basis,
    outer_layer,
    outer_norms,
    outer_embed,
    layer_momentum,
    norm_momentum,
    embed_momentum,
):
    z0, y0 = position()
    outer_rows = outer_embed[0]

    kept = outer_rows - (RATE * MU * MU) * embed_momentum[0]
    half = ROWS // 2
    next_one, last_one = send(kept, shift(-1, 0)), send(kept, shift(1, 0))
    next_two, last_two = send(kept, shift(-2, 0)), send(kept, shift(2, 0))
    next_pair = jnp.concatenate([next_one, next_two[:half]])
    last_pair = jnp.concatenate([last_one, last_two[half:]])
    next_far, last_far = send(next_pair, shift(-2, 0)), send(last_pair, shift(2, 0))
    far = jnp.concatenate([next_far[ROWS:], last_far[ROWS:]])
    embed_own = jnp.stack([kept, next_one, next_two, next_far[:ROWS], far, last_far[:ROWS], last_two, last_one])
    embed_up, embed_down = send(embed_own, shift(0, -1)), send(embed_own, shift(0, 1))
    embed_low = send(embed_up[: Z // 2], shift(0, -1))
    embed_high = send(embed_down[Z // 2 :], shift(0, 1))

    own, *away = pack(inner_columns[0], inner_rows[0], inner_norms.transpose(1, 0, 2), inner_embed[0].T, basis.T)
    came = [send(m, moves(step)) for m, step in zip(away, (swap_one, swap_two, swap_three))]
    base = jnp.dot(outer_rows, basis, precision=HI, preferred_element_type=jnp.float32)
    base = jnp.concatenate([base[: ROWS // 2], base[ROWS // 2 :]], 1)
    base, _, _ = lax.optimization_barrier((base, next_pair, last_pair))
    norm_part = outer_norms - RATE * ((1 + MU) * outer_norms + MU * MU * norm_momentum)
    own, new_layer_m, factor, mean = update(
        own,
        *came,
        outer_layer.reshape(LAYER_TILES, 128),
        layer_momentum.reshape(LAYER_TILES, 128),
        base,
        jnp.pad(norm_part, (0, 128 - NORM))[None],
    )
    factor = jnp.concatenate([factor[:, :RANK], factor[:, RANK:]], 0)
    new_embed_m = MU * embed_momentum[0] + jnp.dot(
        factor, basis.T, precision=HI, preferred_element_type=jnp.float32
    )
    norm_mean = mean[:15].reshape(3, 640)[:, :WIDTH].reshape(-1)
    mine = lax.dynamic_slice(norm_mean, (index_of(z0, y0) * NORM,), (NORM,))
    new_norm_m = MU * norm_momentum + (outer_norms - mine)

    unit = jnp.stack([own, *(send(own, shift(0, -k)) for k in range(1, Y))])
    ups, downs = [], []
    up = down = unit
    for k in range(1, Z // 2):
        up, down = send(up, shift(-1, 0)), send(down, shift(1, 0))
        ups.append(up)
        downs.append(down)
    low, high = send(up[: Y // 2], shift(-1, 0)), send(down[Y // 2 :], shift(1, 0))
    rest = place_embed(embed_own, embed_up, embed_low, embed_high, embed_down)
    new_columns, new_rows, new_norms, new_embed = finish(
        (unit, *ups, low, high, *downs[::-1]), rest, basis, mean
    )
    return (
        new_columns,
        new_rows,
        new_norms,
        new_embed.T,
        new_layer_m.reshape(1, -1),
        new_norm_m,
        new_embed_m[None, :, :],
    )


def solution(mesh):
    in_specs = (
        P("group", None, "mp"),
        P("group", "mp", None),
        P("group", None, None),
        P("group", "mp", None),
        P(),
        P("mp", AXES),
        P(AXES),
        P("mp", AXES, None),
        P("mp", AXES),
        P(AXES),
        P("mp", AXES, None),
    )
    out_specs = (
        P(None, "mp"),
        P("mp", None),
        P(),
        P("mp", None),
        P("mp", AXES),
        P(AXES),
        P("mp", AXES, None),
    )
    return jax.shard_map(local, mesh=mesh, in_specs=in_specs, out_specs=out_specs, check_vma=False)
```

```python
import jax
import jax.numpy as jnp
from jax import lax
from jax.experimental import pallas as pl
from jax.experimental.pallas import tpu as pltpu
from jax.sharding import PartitionSpec as P


MU = 0.5
RATE = 0.7
HI = lax.Precision.HIGHEST
AXES = ("group", "dp")

G, Y, L = 4, 4, 2
Z = G * L
PIECES = G * Y * L
FLAT = 13824
RANK = 64
ROWS = 32
WIDTH = 576
NORM = 54
LAYER_TILES = FLAT // 128
FACTOR_TILES = ROWS * RANK // 128
PIECE = 128
NORM_AT = FACTOR_TILES + LAYER_TILES
MESSAGE = 144
NORM_LINES = 14
COL_WIDTH = 504
ROW_HEIGHT = 264
COL_TILES = WIDTH * COL_WIDTH // 128


def index_of(z, y):
    return (z // L) % G * (Y * L) + y % Y * L + z % L


def position():
    place = lax.axis_index("dp")
    return lax.axis_index("group") * L + lax.rem(place, L), place // L


def moves(step):
    pairs = []
    for z in range(Z):
        for y in range(Y):
            tz, ty = step(z, y)
            pairs.append((index_of(z, y), index_of(tz % Z, ty % Y)))
    return pairs


def swap_one(z, y):
    return (z + 1, y) if z % 2 else (z - 1, y)


def swap_two(z, y):
    return (z + 2, y) if z % 2 else (z - 2, y)


def swap_three(z, y):
    return (z + 3, y) if z % 2 else (z - 3, y)


def shift(dz, dy):
    return moves(lambda z, y: (z + dz, y + dy))


def send(value, pairs):
    return lax.ppermute(value, AXES, pairs)


def segments(start, width):
    found, at = [], 0
    while at < 128:
        row, column = divmod(start + at, width)
        tile, lane = divmod(column, 128)
        count = min(128 - at, 128 - lane, width - column)
        found.append((row, tile, lane, at, count))
        at += count
    return found


def join(parts):
    out = None
    for value, lane, at, count in parts:
        turn = (at - lane) % 128
        value = pltpu.roll(value, turn, 1) if turn else value
        if out is None:
            out = value
        else:
            lanes = lax.broadcasted_iota(jnp.int32, value.shape, 1)
            out = jnp.where(lanes >= at, value, out)
    return out


def flatten(tiles, flat, base, width, period, groups):
    made = period * width // 128
    for j in range(made):
        flat[pl.ds(base + j, groups, stride=made), :] = join(
            [
                (tiles[tile, pl.ds(row, groups, stride=period), :], lane, at, count)
                for row, tile, lane, at, count in segments(128 * j, width)
            ]
        )


def unflatten(flat, base, tiles, width, period, groups):
    made = period * width // 128
    for row in range(period):
        for tile in range((width + 127) // 128):
            start = row * width + tile * 128
            line, lane = divmod(start, 128)
            count = min(128, width - tile * 128)
            parts = [(flat[pl.ds(base + line, groups, stride=made), :], lane, 0, 128 - lane)]
            if 128 - lane < count:
                parts.append((flat[pl.ds(base + line + 1, groups, stride=made), :], 0, 128 - lane, lane))
            tiles[tile, pl.ds(row, groups, stride=period), :] = join(parts)


def to_tiles(rows, tiles):
    width = rows.shape[1]
    for tile in range(tiles.shape[0]):
        count = min(128, width - tile * 128)
        tiles[tile, pl.ds(0, rows.shape[0]), pl.ds(0, count)] = rows[:, pl.ds(tile * 128, count)]


def from_tiles(tiles, rows):
    width = rows.shape[1]
    for tile in range(tiles.shape[0]):
        count = min(128, width - tile * 128)
        rows[:, pl.ds(tile * 128, count)] = tiles[tile, pl.ds(0, rows.shape[0]), pl.ds(0, count)]


def pack_kernel(columns, rows, norms, embed_t, basis_t, *refs):
    messages = refs[:4]
    cbuf, rbuf, ebuf, ctiles, rtiles, ntiles, flat, sem = refs[4:]
    z0, y0 = position()
    away = 2 * lax.rem(z0, L) - 1
    pieces = [index_of(lax.rem(z0 + k * away + Z, Z), y0) for k in range(G)]
    copies = [pltpu.make_async_copy(columns, cbuf, sem.at[0]), pltpu.make_async_copy(rows, rbuf, sem.at[1])]
    for k, p in enumerate(pieces):
        at = pl.ds(pl.multiple_of(p // 4 * 128, 128), 128)
        copies.append(pltpu.make_async_copy(embed_t.at[:, at], ebuf.at[k], sem.at[2 + k]))
    for copy in copies:
        copy.start()
    copies[0].wait()
    to_tiles(cbuf, ctiles)
    flatten(ctiles, flat, 0, COL_WIDTH, 16, WIDTH // 16)
    copies[1].wait()
    to_tiles(rbuf, rtiles)
    flatten(rtiles, flat, COL_TILES, WIDTH, 2, ROW_HEIGHT // 2)
    for copy in copies[2:]:
        copy.wait()
    picked = None
    lanes = lax.broadcasted_iota(jnp.int32, (WIDTH, 128), 1)
    for k, p in enumerate(pieces):
        turned = pltpu.roll(ebuf[k], lax.rem(k * ROWS + 128 - lax.rem(p, 4) * ROWS, 128), 1)
        picked = turned if picked is None else jnp.where(lanes >= k * ROWS, turned, picked)
    projected = jnp.dot(basis_t[...], picked, precision=HI, preferred_element_type=jnp.float32).T
    for row in range(3):
        for tile in range(5):
            count = min(128, WIDTH - tile * 128)
            ntiles[tile, pl.ds(row, 1), pl.ds(0, count)] = norms[row, :, pl.ds(tile * 128, count)]
    lines = []
    for line in range(NORM_LINES):
        parts = [part for part in segments(128 * line, WIDTH) if part[0] < 3]
        lines.append(join([(ntiles[tile, pl.ds(row, 1), :], lane, at, count) for row, tile, lane, at, count in parts]))
    for k, (p, message) in enumerate(zip(pieces, messages)):
        message[pl.ds(0, FACTOR_TILES), :] = jnp.concatenate(
            [projected[k * ROWS : k * ROWS + 16], projected[k * ROWS + 16 : (k + 1) * ROWS]], 1
        )
        message[pl.ds(FACTOR_TILES, LAYER_TILES), :] = flat[pl.ds(p * LAYER_TILES, LAYER_TILES), :]
        message[pl.ds(NORM_AT, MESSAGE - NORM_AT), :] = jnp.zeros((MESSAGE - NORM_AT, 128), jnp.float32)
        for line in range(NORM_LINES):
            message[pl.ds(NORM_AT + line, 1), :] = lines[line]


VMEM = pl.BlockSpec(memory_space=pltpu.VMEM)
ANY = pl.BlockSpec(memory_space=pl.ANY)


def f32(*shape):
    return jax.ShapeDtypeStruct(shape, jnp.float32)


def pack(columns, rows, norms, embed_t, basis_t):
    return pl.pallas_call(
        pack_kernel,
        out_shape=(f32(MESSAGE, 128),) * 4,
        in_specs=[ANY, ANY, VMEM, ANY, VMEM],
        out_specs=(VMEM,) * 4,
        scratch_shapes=[
            pltpu.VMEM(columns.shape, jnp.float32),
            pltpu.VMEM(rows.shape, jnp.float32),
            pltpu.VMEM((G, WIDTH, 128), jnp.float32),
            pltpu.VMEM((4, 640, 128), jnp.float32),
            pltpu.VMEM((5, 272, 128), jnp.float32),
            pltpu.VMEM((5, 8, 128), jnp.float32),
            pltpu.VMEM((3496, 128), jnp.float32),
            pltpu.SemaphoreType.DMA((6,)),
        ],
        compiler_params=pltpu.CompilerParams(vmem_limit_bytes=60 << 20),
        name="pack",
    )(columns, rows, norms, embed_t, basis_t)


def update_kernel(own, one, two, three, weights, momentum, base, norms, piece, fresh_out, factor_out, mean_out, norm_out):
    mean = (own[...] + one[...] + two[...] + three[...]) * (1 / G)
    factor = base[...] - mean[:FACTOR_TILES]
    delta = weights[...] - mean[FACTOR_TILES:NORM_AT]
    fresh = MU * momentum[...] + delta
    piece[pl.ds(0, FACTOR_TILES), :] = factor
    piece[pl.ds(FACTOR_TILES, LAYER_TILES), :] = weights[...] - RATE * (delta + MU * fresh)
    piece[pl.ds(NORM_AT, PIECE - NORM_AT), :] = jnp.zeros((PIECE - NORM_AT, 128), jnp.float32)
    norm, speed = norms[pl.ds(0, 1), :], norms[pl.ds(1, 1), :]
    piece[pl.ds(NORM_AT, 1), :] = norm - RATE * ((1 + MU) * norm + MU * MU * speed)
    fresh_out[...] = fresh
    factor_out[...] = factor
    mean_out[...] = mean[NORM_AT:]
    start = index_of(*position()) * NORM
    line, lane = start // 128, lax.rem(start, 128)
    turn = lax.rem(128 - lane, 128)
    lanes = lax.broadcasted_iota(jnp.int32, (1, 128), 1)
    mine = jnp.where(
        lanes < 128 - lane,
        pltpu.roll(mean_out[pl.ds(line, 1), :], turn, 1),
        pltpu.roll(mean_out[pl.ds(line + 1, 1), :], turn, 1),
    )
    norm_out[...] = MU * speed + (norm - mine)


def update(*args):
    return pl.pallas_call(
        update_kernel,
        out_shape=(
            f32(PIECE, 128),
            f32(LAYER_TILES, 128),
            f32(FACTOR_TILES, 128),
            f32(MESSAGE - NORM_AT, 128),
            f32(1, 128),
        ),
        in_specs=[VMEM] * 8,
        out_specs=(VMEM,) * 5,
        compiler_params=pltpu.CompilerParams(vmem_limit_bytes=3 << 20),
        name="update",
    )(*args)


def place_embed_kernel(own, up, half_low, half_high, down, out, rows):
    z0, y0 = position()

    def put(ref, at, zk, yk):
        p = index_of(lax.rem(z0 + zk, Z), lax.rem(y0 + yk, Y))
        rows[pl.ds(pl.multiple_of(p * ROWS, ROWS), ROWS), :] = ref[at]

    for zk in range(Z):
        put(own, zk, zk, 0)
        put(up, zk, zk, 1)
        put(half_low if zk < 4 else half_high, zk % 4, zk, 2)
        put(down, zk, zk, 3)
    for b in range(PIECES * ROWS // 128):
        at = pl.ds(b * 128, 128)
        out[:, at] = rows[at, :].T


def place_embed(*units):
    return pl.pallas_call(
        place_embed_kernel,
        out_shape=f32(WIDTH, PIECES * ROWS),
        in_specs=[VMEM] * 5,
        out_specs=VMEM,
        scratch_shapes=[pltpu.VMEM((PIECES * ROWS, WIDTH), jnp.float32)],
        compiler_params=pltpu.CompilerParams(vmem_limit_bytes=12 << 20),
        name="place_embed",
    )(*units)


def split(value):
    high = value.astype(jnp.bfloat16)
    return high, (value - high.astype(jnp.float32)).astype(jnp.bfloat16)


def finish_kernel(*refs):
    units, (rest, basis, mean) = refs[:9], refs[9:12]
    columns_out, rows_out, norms_out, embed_out = refs[12:16]
    flat, factor, norm, ctiles, rtiles, cbuf, rbuf, ebuf, sem = refs[16:]
    z0, y0 = position()

    def put(ref, at, zk, yk):
        p = index_of(lax.rem(z0 + zk, Z), lax.rem(y0 + yk, Y))
        flat[pl.ds(p * LAYER_TILES, LAYER_TILES), :] = ref[at, pl.ds(FACTOR_TILES, LAYER_TILES), :]
        packed = ref[at, pl.ds(0, FACTOR_TILES), :]
        factor[pl.ds(pl.multiple_of(p * ROWS, ROWS), ROWS), :] = jnp.concatenate(
            [packed[:, :RANK], packed[:, RANK:]], 0
        )
        norm[pl.ds(p, 1), :] = ref[at, pl.ds(NORM_AT, 1), :]

    for zk in range(Z):
        for yk in range(Y):
            if zk == Z // 2:
                put(units[4 if yk < 2 else 5], yk % 2, zk, yk)
            else:
                put(units[zk if zk < 4 else zk + 1], yk, zk, yk)

    high, low = split(factor[...])
    right = jnp.concatenate([high, high, low, low], 1)
    high, low = split(basis[...] * (RATE * (1 + MU)))
    left = jnp.concatenate([high, low, high, low], 1)
    ebuf[...] = rest[...] - lax.dot_general(
        left, right, (((1,), (1,)), ((), ())), preferred_element_type=jnp.float32
    )
    embed_copy = pltpu.make_async_copy(ebuf, embed_out, sem.at[0])
    embed_copy.start()
    unflatten(flat, 0, ctiles, COL_WIDTH, 16, WIDTH // 16)
    from_tiles(ctiles, cbuf)
    columns_copy = pltpu.make_async_copy(cbuf, columns_out, sem.at[1])
    columns_copy.start()
    unflatten(flat, COL_TILES, rtiles, WIDTH, 2, ROW_HEIGHT // 2)
    from_tiles(rtiles, rbuf)
    rows_copy = pltpu.make_async_copy(rbuf, rows_out, sem.at[2])
    rows_copy.start()
    for row in range(3):
        for tile in range(5):
            start, count = row * WIDTH + tile * 128, min(128, WIDTH - tile * 128)
            parts, at = [], 0
            while at < count:
                p, lane = divmod(start + at, NORM)
                size = min(count - at, NORM - lane)
                parts.append((norm[pl.ds(p, 1), :], lane, at, size))
                at += size
            line, lane = divmod(start, 128)
            mean_parts = [(mean[pl.ds(line, 1), :], lane, 0, 128 - lane)]
            if 128 - lane < count:
                mean_parts.append((mean[pl.ds(line + 1, 1), :], 0, 128 - lane, lane))
            value = join(parts) + (RATE * (1 + MU)) * join(mean_parts)
            norms_out[pl.ds(row, 1), pl.ds(tile * 128, count)] = value[:, :count]
    embed_copy.wait()
    columns_copy.wait()
    rows_copy.wait()


def finish(units, rest, basis, mean):
    return pl.pallas_call(
        finish_kernel,
        out_shape=(
            f32(WIDTH, COL_WIDTH),
            f32(ROW_HEIGHT, WIDTH),
            f32(3, WIDTH),
            f32(WIDTH, PIECES * ROWS),
        ),
        in_specs=[VMEM] * 12,
        out_specs=(ANY, ANY, VMEM, ANY),
        scratch_shapes=[
            pltpu.VMEM((3496, 128), jnp.float32),
            pltpu.VMEM((PIECES * ROWS, RANK), jnp.float32),
            pltpu.VMEM((PIECES, 128), jnp.float32),
            pltpu.VMEM((4, 640, 128), jnp.float32),
            pltpu.VMEM((5, 272, 128), jnp.float32),
            pltpu.VMEM((WIDTH, COL_WIDTH), jnp.float32),
            pltpu.VMEM((ROW_HEIGHT, WIDTH), jnp.float32),
            pltpu.VMEM((WIDTH, PIECES * ROWS), jnp.float32),
            pltpu.SemaphoreType.DMA((3,)),
        ],
        compiler_params=pltpu.CompilerParams(vmem_limit_bytes=18 << 20),
        name="finish",
    )(*units, rest, basis, mean)


def local(
    inner_columns,
    inner_rows,
    inner_norms,
    inner_embed,
    basis,
    outer_layer,
    outer_norms,
    outer_embed,
    layer_momentum,
    norm_momentum,
    embed_momentum,
):
    z0, y0 = position()
    outer_rows = outer_embed[0]

    own, *away = pack(inner_columns[0], inner_rows[0], inner_norms.transpose(1, 0, 2), inner_embed[0].T, basis.T)
    came = [send(m, moves(step)) for m, step in zip(away, (swap_one, swap_two, swap_three))]

    outer_rows, _ = lax.optimization_barrier((outer_rows, away[0]))
    kept = outer_rows - (RATE * MU * MU) * embed_momentum[0]
    half = ROWS // 2
    next_one, last_one = send(kept, shift(-1, 0)), send(kept, shift(1, 0))
    next_two, last_two = send(kept, shift(-2, 0)), send(kept, shift(2, 0))
    next_pair = jnp.concatenate([next_one, next_two[:half]])
    last_pair = jnp.concatenate([last_one, last_two[half:]])
    next_far, last_far = send(next_pair, shift(-2, 0)), send(last_pair, shift(2, 0))
    far = jnp.concatenate([next_far[ROWS:], last_far[ROWS:]])
    embed_own = jnp.stack([kept, next_one, next_two, next_far[:ROWS], far, last_far[:ROWS], last_two, last_one])
    embed_up, embed_down = send(embed_own, shift(0, -1)), send(embed_own, shift(0, 1))
    embed_low = send(embed_up[: Z // 2], shift(0, -1))
    embed_high = send(embed_down[Z // 2 :], shift(0, 1))

    base = jnp.dot(outer_rows, basis, precision=HI, preferred_element_type=jnp.float32)
    base = jnp.concatenate([base[: ROWS // 2], base[ROWS // 2 :]], 1)
    own, new_layer_m, factor, mean, new_norm_m = update(
        own,
        *came,
        outer_layer.reshape(LAYER_TILES, 128),
        layer_momentum.reshape(LAYER_TILES, 128),
        base,
        jnp.pad(jnp.stack([outer_norms, norm_momentum]), ((0, 0), (0, 128 - NORM))),
    )
    factor = jnp.concatenate([factor[:, :RANK], factor[:, RANK:]], 0)
    new_embed_m = MU * embed_momentum[0] + jnp.dot(
        factor, basis.T, precision=HI, preferred_element_type=jnp.float32
    )
    unit = jnp.stack([own, *(send(own, shift(0, -k)) for k in range(1, Y))])
    ups, downs = [], []
    up = down = unit
    for _ in range(1, Z // 2):
        up, down = send(up, shift(-1, 0)), send(down, shift(1, 0))
        ups.append(up)
        downs.append(down)
    low, high = send(up[: Y // 2], shift(-1, 0)), send(down[Y // 2 :], shift(1, 0))
    rest = place_embed(embed_own, embed_up, embed_low, embed_high, embed_down)
    new_columns, new_rows, new_norms, new_embed = finish(
        (unit, *ups, low, high, *downs[::-1]), rest, basis, mean
    )
    return (
        new_columns,
        new_rows,
        new_norms,
        new_embed.T,
        new_layer_m.reshape(1, -1),
        new_norm_m[0, :NORM],
        new_embed_m[None, :, :],
    )


def solution(mesh):
    in_specs = (
        P("group", None, "mp"),
        P("group", "mp", None),
        P("group", None, None),
        P("group", "mp", None),
        P(),
        P("mp", AXES),
        P(AXES),
        P("mp", AXES, None),
        P("mp", AXES),
        P(AXES),
        P("mp", AXES, None),
    )
    out_specs = (
        P(None, "mp"),
        P("mp", None),
        P(),
        P("mp", None),
        P("mp", AXES),
        P(AXES),
        P("mp", AXES, None),
    )

    return jax.shard_map(local, mesh=mesh, in_specs=in_specs, out_specs=out_specs, check_vma=False)
```
